32 devices in a mesh: groups: 2 (over y), expert: 4 (over z), dp: 4 (over x, core).
Axes of the slice: x: 2, y: 2, z: 4, core: 2. Of those that a mesh axis runs over, the one named last changes fastest.
Arguments:
- tokens: bfloat16 [4096, 1024], P(('groups', 'expert', 'dp')), parts along dimension 0, may hold values from -6 to 6
- expert_ids: int32 [4096, 8], P(('groups', 'expert', 'dp')), parts along dimension 0, may hold values from 0 to 63, all different within a row; in each aligned block of 128 rows (0 to 127, 128 to 255, ...) at most 16 rows name the same one
- gate_values: float32 [4096, 8], P(('groups', 'expert', 'dp')), parts along dimension 0, may hold values from 0.1 to 1
- w_gate_up: bfloat16 [64, 1024, 768], P('expert', 'dp'), may hold values from -0.1875 to 0.1875
- w_down: bfloat16 [64, 384, 1024], P('expert', None, 'dp'), may hold values from -0.3125 to 0.3125
- new_slot: int32 [64], replicated, may hold values from 0 to 63, each once
- cotangent: bfloat16 [4096, 1024], P(('groups', 'expert', 'dp')), parts along dimension 0, may hold values from -6 to 6
Outputs:
- layer_out: bfloat16 [4096, 1024], P(('groups', 'expert', 'dp')), parts along dimension 0
- d_tokens: bfloat16 [4096, 1024], P(('groups', 'expert', 'dp')), parts along dimension 0
- d_gate_up: bfloat16 [128, 1024, 768], P(('groups', 'expert'), 'dp'), parts along dimension 0
- d_down: bfloat16 [128, 384, 1024], P(('groups', 'expert'), None, 'dp'), parts along dimension 0
The draws below stay inside these ranges and needn't reach their ends.
There are 2 independent parts, one for each index of `groups`. The reference program is written for one: setup_inputs(seed, part) draws one part's arguments, and reference() takes and returns one part's arrays. A program takes and returns all parts, laid end to end along the dimension named above; an argument that names none is the same for every part. Nothing has to cross between parts.
Inputs may be any that keep to these rules, and one draw needn't show every extreme that they name: `expert_ids`: each row names 8 different experts; among the 128 rows of one device no expert is named by more than 16 rows, and on some devices some expert is named by exactly 16. `new_slot`: every number appears once, so each slot holds one expert; slot s belongs to index s // (64 / 4) of axis expert.
All inputs are finite; a program needn't handle non-finite values.
Results may differ from the reference program's by a relative error of at most 0.0095.
Values may be sent and summed in bfloat16 or wider, within the bound.
No kernel may reach another device: no remote copies, remote signals or barrier semaphores. Data moves between devices by JAX's collectives and lax.ppermute only.
A program may use at most 192 MiB of HBM per device.

```python
import math
from functools import partial
import jax
import jax.numpy as jnp
import numpy as np
from jax import lax

D = 1024
FF = 384
EXPERTS = 64
TOP = 8
TOK_DEV = 128
MOST = 16
TOKENS = 2048
N_EXPERT = 4
N_DP = 4


def block_levels(stream_key, shape, pieces, low, high):
    level = 1.0
    for axis_at, shards_of in pieces:
        steps = jax.random.uniform(jax.random.fold_in(jax.random.fold_in(stream_key, 6), axis_at), (shards_of,), jnp.float32, low / len(pieces), high / len(pieces))
        level = level * jnp.repeat(jnp.exp(steps), shape[axis_at] // shards_of).reshape((-1,) + (1,) * (len(shape) - 1 - axis_at))
    return level


def shared_out(key, own, number, rows, count, top, limit, slope):
    ranking = jax.random.permutation(key, count)
    packed, ordinary = portions_of(count, rows * top, limit, slope, True), portions_of(count, rows * top, limit, slope, False)
    places = jnp.arange(count)

    def named(sizes, rotation):
        used = int((sizes > 0).sum())
        fixed = max(1, used // 4)
        passed = fixed + (places - fixed + rotation * (used - fixed)) % max(1, count - fixed)
        return jnp.zeros((count,), jnp.int32).at[ranking[jnp.where(places < fixed, places, passed)]].set(jnp.asarray(sizes, jnp.int32))

    sizes = jnp.where(number % 4 == 0, named(packed, number // 4), named(ordinary, number - number // 4 - 1))
    mixed = jax.random.permutation(jax.random.fold_in(own, 3), count)
    giver, receiver = mixed[0:count // 2 * 2:2], mixed[1:count // 2 * 2:2]
    slack = jnp.minimum(sizes[giver] - 1, limit - sizes[receiver]) // 2
    slack = jnp.where((giver == ranking[0]) | (receiver == ranking[0]) | (sizes[receiver] == 0), 0, jnp.maximum(slack, 0))
    passed = jax.random.randint(jax.random.fold_in(own, 4), (count // 2,), 0, 1 << 20) % (slack + 1)
    sizes = sizes.at[giver].add(-passed).at[receiver].add(passed)
    items = jnp.searchsorted(jnp.cumsum(sizes), jnp.arange(rows * top), side="right").astype(jnp.int32)
    grid = items.reshape(top, rows).T
    grid = grid[jax.random.permutation(jax.random.fold_in(own, 1), rows)]
    rotation = jax.random.randint(jax.random.fold_in(own, 2), (rows, 1), 0, top)
    return jnp.take_along_axis(grid, (jnp.arange(top)[None, :] + rotation) % top, axis=1)


def portions_of(amount, total, bound, skew, full):
    portions = [(1 << 20) // math.isqrt(standing ** skew) + 1 for standing in range(1, amount + 1)]
    largest = bound if full else min(bound, max(-(-total // amount), total * portions[0] // sum(portions)))
    least = 1 if total - largest >= amount - 1 else 0
    holding, spare = [largest] + [least] * (amount - 1), total - largest - least * (amount - 1)
    while spare > 0:
        movable = [i for i in range(1, amount) if holding[i] < largest] or [i for i in range(1, amount) if holding[i] < bound]
        mass, remaining = sum([portions[i] for i in movable]), spare
        for i in movable:
            extra = min(bound - holding[i], max(1, remaining * portions[i] // mass), spare)
            holding[i] = holding[i] + extra
            spare = spare - extra
    return np.array(holding)


def normal_values(stream_key, extent, scale, bound, shards=(), held_as=jnp.bfloat16):
    result = scale * jax.random.normal(stream_key, extent, jnp.float32)
    if shards:
        result = result * block_levels(stream_key, extent, shards, -0.22, 0.18)
    return jnp.clip(result, -bound, bound).astype(held_as)


def setup_inputs(seed: int = 0, part: int = 0) -> dict:
    arg_keys = jax.random.split(jax.random.key(seed), 8)
    own_keys = jax.random.split(jax.random.fold_in(arg_keys[7], part), 8)
    tokens = normal_values(own_keys[0], (TOKENS, D), 1.0, 6.0, ((0, 16),))
    expert_ids_keys = jax.random.split(jax.random.fold_in(own_keys[1], 1), TOKENS // TOK_DEV)
    expert_ids_turns = jax.random.permutation(jax.random.fold_in(own_keys[1], 3), TOKENS // TOK_DEV)
    expert_ids = jax.vmap(lambda own, number: shared_out(jax.random.fold_in(own_keys[1], 2), own, number, TOK_DEV, EXPERTS, TOP, MOST, 2))(expert_ids_keys, expert_ids_turns).reshape((TOKENS, TOP))
    gate_values = jnp.clip(0.1 + 0.9 * jax.random.uniform(own_keys[2], (TOKENS, TOP), jnp.float32) ** block_levels(own_keys[2], (TOKENS, TOP), ((0, 16),), -0.2, 0.2), 0.1, 1.0)
    w_gate_up = normal_values(arg_keys[3], (EXPERTS, D, 2 * FF), D ** -0.5, 0.1875, ((0, 4), (1, 4)))
    w_down = normal_values(arg_keys[4], (EXPERTS, FF, D), FF ** -0.5, 0.3125, ((0, 4), (2, 4)))
    new_slot = jax.random.permutation(arg_keys[5], EXPERTS).astype(jnp.int32)
    cotangent = normal_values(own_keys[6], (TOKENS, D), 1.0, 6.0, ((0, 16),))
    return dict(tokens=tokens, expert_ids=expert_ids, gate_values=gate_values, w_gate_up=w_gate_up, w_down=w_down, new_slot=new_slot, cotangent=cotangent)


def route_table(expert_ids):
    flat_ids = expert_ids.reshape(-1)
    matches = flat_ids[:, None] == jnp.arange(EXPERTS, dtype=jnp.int32)[None, :]
    indicator = matches.astype(jnp.int32)
    earlier = jnp.cumsum(indicator, axis=0) - indicator
    position = jnp.sum(jnp.where(matches, earlier, 0), axis=1).astype(jnp.int32)
    target_cell = (flat_ids * MOST + position).astype(jnp.int32)
    entries = flat_ids.shape[0]
    table = jnp.full((EXPERTS * MOST,), entries, jnp.int32).at[target_cell].set(jnp.arange(entries, dtype=jnp.int32))
    return table.reshape(EXPERTS, MOST)


def expert_step(padded_tokens, padded_cot, carry, inputs):
    out_sum, grad_sum = carry
    rows_index, gate_cells, weight_gu, weight_dn = inputs
    flat_index = rows_index.reshape(-1)
    gate_flat = gate_cells.reshape(-1)
    arrived = padded_tokens[flat_index]
    cot_rows = padded_cot[flat_index]
    gate_up = jnp.dot(arrived, weight_gu, preferred_element_type=jnp.float32)
    gate_part = gate_up[:, :FF]
    up_part = gate_up[:, FF:]
    sigmoid_g = jax.nn.sigmoid(gate_part)
    silu_g = gate_part * sigmoid_g
    activation = (silu_g * up_part).astype(jnp.bfloat16)
    expert_out = jnp.dot(activation, weight_dn, preferred_element_type=jnp.float32).astype(jnp.bfloat16)
    out_sum = out_sum.at[flat_index].add(gate_flat[:, None] * expert_out.astype(jnp.float32))
    d_outputs = (gate_flat[:, None] * cot_rows.astype(jnp.float32)).astype(jnp.bfloat16)
    d_act = jnp.dot(d_outputs, weight_dn.T, preferred_element_type=jnp.float32)
    d_gate = d_act * up_part * sigmoid_g * (1.0 + gate_part * (1.0 - sigmoid_g))
    d_up = d_act * silu_g
    d_gate_up = jnp.concatenate([d_gate, d_up], axis=1).astype(jnp.bfloat16)
    d_rows = jnp.dot(d_gate_up, weight_gu.T, preferred_element_type=jnp.float32).astype(jnp.bfloat16)
    grad_sum = grad_sum.at[flat_index].add(d_rows.astype(jnp.float32))
    x_four = arrived.reshape(N_EXPERT, N_DP, MOST, D).astype(jnp.float32)
    g_four = d_gate_up.reshape(N_EXPERT, N_DP, MOST, 2 * FF).astype(jnp.float32)
    a_four = activation.reshape(N_EXPERT, N_DP, MOST, FF).astype(jnp.float32)
    o_four = d_outputs.reshape(N_EXPERT, N_DP, MOST, D).astype(jnp.float32)
    part_gu = jnp.einsum("ijmd,ijmf->jdf", x_four, g_four)
    part_dn = jnp.einsum("ijmf,ijmd->jfd", a_four, o_four)
    rounded_gu = lax.optimization_barrier(part_gu.astype(jnp.bfloat16))
    rounded_dn = lax.optimization_barrier(part_dn.astype(jnp.bfloat16))
    grad_gu = jnp.sum(rounded_gu.astype(jnp.float32), axis=0).astype(jnp.bfloat16)
    grad_dn = jnp.sum(rounded_dn.astype(jnp.float32), axis=0).astype(jnp.bfloat16)
    return (out_sum, grad_sum), (grad_gu, grad_dn)


def reference(tokens, expert_ids, gate_values, w_gate_up, w_down, new_slot, cotangent):
    devices = N_EXPERT * N_DP
    entries = TOK_DEV * TOP
    tables = jax.vmap(route_table)(expert_ids.reshape(devices, TOK_DEV, TOP))
    valid = tables < entries
    device_base = (jnp.arange(devices, dtype=jnp.int32) * TOK_DEV)[:, None, None]
    row_index = jnp.where(valid, device_base + tables // TOP, TOKENS).astype(jnp.int32)
    gate_flat = gate_values.reshape(devices, entries)
    clipped = jnp.minimum(tables, entries - 1).reshape(devices, -1).astype(jnp.int32)
    picked = jnp.take_along_axis(gate_flat, clipped, axis=1).reshape(tables.shape)
    gate_cells = jnp.where(valid, picked, jnp.zeros_like(picked))
    blank_row = jnp.zeros((1, D), tokens.dtype)
    padded_tokens = jnp.concatenate([tokens, blank_row], axis=0)
    padded_cot = jnp.concatenate([cotangent, blank_row], axis=0)
    inputs = (jnp.swapaxes(row_index, 0, 1), jnp.swapaxes(gate_cells, 0, 1), w_gate_up, w_down)
    start = (jnp.zeros((TOKENS + 1, D), jnp.float32), jnp.zeros((TOKENS + 1, D), jnp.float32))
    stepper = partial(expert_step, padded_tokens, padded_cot)
    (out_sum, grad_sum), (grads_gu, grads_dn) = lax.scan(stepper, start, inputs)
    layer_out = out_sum[:TOKENS].astype(jnp.bfloat16)
    d_tokens = grad_sum[:TOKENS].astype(jnp.bfloat16)
    d_gate_up = jnp.zeros_like(grads_gu).at[new_slot].set(grads_gu)
    d_down = jnp.zeros_like(grads_dn).at[new_slot].set(grads_dn)
    return (layer_out, d_tokens, d_gate_up, d_down)
```

```python
import functools

import jax
import jax.numpy as jnp
from jax import lax
from jax.experimental import pallas as pl
from jax.experimental.pallas import tpu as pltpu
from jax.sharding import PartitionSpec as P

MOST = 16


def relocate(gate_up, down, inverse):
    expert_peers = lax.axis_size("expert")
    home_slots = gate_up.shape[0]
    spread_gu = gate_up.reshape(
        home_slots, expert_peers, gate_up.shape[1] // expert_peers, gate_up.shape[2]
    )
    spread_dn = down.reshape(home_slots, expert_peers, down.shape[1] // expert_peers, down.shape[2])
    got_gu, got_dn = (
        lax.all_to_all(spread_gu, "expert", split_axis=1, concat_axis=0, tiled=True),
        lax.all_to_all(spread_dn, "expert", split_axis=1, concat_axis=0, tiled=True),
    )
    experts = home_slots * expert_peers
    slot_order = inverse.reshape(expert_peers, home_slots).T
    pick_gu = got_gu.reshape(experts, got_gu.shape[2], got_gu.shape[3])[slot_order]
    pick_dn = got_dn.reshape(experts, got_dn.shape[2], got_dn.shape[3])[slot_order]
    new_gu, new_dn = (
        lax.all_to_all(pick_gu, "expert", split_axis=1, concat_axis=1, tiled=True),
        lax.all_to_all(pick_dn, "expert", split_axis=1, concat_axis=1, tiled=True),
    )
    return (new_gu.reshape(gate_up.shape), new_dn.reshape(down.shape))


def route_cells(expert_ids, slot_map):
    experts = slot_map.shape[0]
    flat_ids = expert_ids.reshape(-1)
    matches = flat_ids[:, None] == jnp.arange(experts, dtype=jnp.int32)[None, :]
    indicator = matches.astype(jnp.int32)
    earlier = jnp.cumsum(indicator, axis=0) - indicator
    position = jnp.sum(jnp.where(matches, earlier, 0), axis=1)
    target = jnp.sum(jnp.where(matches, slot_map[None, :], 0), axis=1)
    target_cell = target * MOST + position
    entries = flat_ids.shape[0]
    source = (
        jnp.full((experts * MOST,), entries, jnp.int32)
        .at[target_cell]
        .set(jnp.arange(entries, dtype=jnp.int32))
    )
    return (target_cell, source)


def by_rows(tokens, expert_ids, gate_values, w_gate_up, w_down, new_slot, cotangent):
    expert_peers = lax.axis_size("expert")
    home_slots = w_gate_up.shape[0]
    model_width = tokens.shape[1]
    hidden_width = w_down.shape[1]
    top_count = expert_ids.shape[1]
    token_count = tokens.shape[0]
    inverse = jnp.argsort(new_slot)
    local_gu, local_dn = relocate(w_gate_up, w_down, inverse)
    full_gu, full_dn = (
        lax.all_gather(local_gu, "dp", axis=1, tiled=True),
        lax.all_gather(local_dn, "dp", axis=2, tiled=True),
    )
    target_cell, source = route_cells(expert_ids, new_slot)
    blank_row = jnp.zeros((1, model_width), jnp.bfloat16)
    token_row = source // top_count
    cell_gates = jnp.concatenate([gate_values.reshape(-1), jnp.zeros((1,), jnp.float32)])[source]
    outgoing = jnp.concatenate([tokens, blank_row], axis=0)[token_row]
    cot_rows = jnp.concatenate([cotangent, blank_row], axis=0)[token_row]
    scaled_cot = (cell_gates[:, None] * cot_rows.astype(jnp.float32)).astype(jnp.bfloat16)
    row_shape = (expert_peers, home_slots, MOST, model_width)
    arrived = lax.all_to_all(
        outgoing.reshape(row_shape), "expert", split_axis=0, concat_axis=0, tiled=True
    )
    gate_up = jnp.einsum("shmd,hdf->shmf", arrived, full_gu, preferred_element_type=jnp.float32)
    gate_part = gate_up[..., :hidden_width]
    up_part = gate_up[..., hidden_width:]
    sigmoid_g = jax.nn.sigmoid(gate_part)
    silu_g = gate_part * sigmoid_g
    activation = (silu_g * up_part).astype(jnp.bfloat16)
    expert_out = jnp.einsum(
        "shmf,hfd->shmd", activation, full_dn, preferred_element_type=jnp.float32
    ).astype(jnp.bfloat16)
    returned = lax.all_to_all(expert_out, "expert", split_axis=0, concat_axis=0, tiled=True)
    gathered_out = returned.reshape(-1, model_width)[target_cell].reshape(
        token_count, top_count, model_width
    )
    layer_out = jnp.sum(gate_values[:, :, None] * gathered_out.astype(jnp.float32), axis=1).astype(
        jnp.bfloat16
    )
    d_outputs = lax.all_to_all(
        scaled_cot.reshape(row_shape), "expert", split_axis=0, concat_axis=0, tiled=True
    )
    d_act = jnp.einsum("shmd,hfd->shmf", d_outputs, full_dn, preferred_element_type=jnp.float32)
    d_gate = d_act * up_part * sigmoid_g * (1.0 + gate_part * (1.0 - sigmoid_g))
    d_up = d_act * silu_g
    d_gate_up = jnp.concatenate([d_gate, d_up], axis=-1).astype(jnp.bfloat16)
    d_rows = jnp.einsum(
        "shmf,hdf->shmd", d_gate_up, full_gu, preferred_element_type=jnp.float32
    ).astype(jnp.bfloat16)
    rows_back = lax.all_to_all(d_rows, "expert", split_axis=0, concat_axis=0, tiled=True)
    gathered_grads = rows_back.reshape(-1, model_width)[target_cell].reshape(
        token_count, top_count, model_width
    )
    d_tokens = jnp.sum(gathered_grads.astype(jnp.float32), axis=1).astype(jnp.bfloat16)
    part_gu = jnp.einsum("shmd,shmf->hdf", arrived, d_gate_up, preferred_element_type=jnp.float32)
    part_dn = jnp.einsum(
        "shmd,shmf->hdf", d_outputs, activation, preferred_element_type=jnp.float32
    )
    sum_gu, sum_dn = (
        lax.psum_scatter(
            part_gu.astype(jnp.bfloat16), "dp", scatter_dimension=1, tiled=True
        ).astype(jnp.float32),
        lax.psum_scatter(
            part_dn.astype(jnp.bfloat16), "dp", scatter_dimension=1, tiled=True
        ).astype(jnp.float32),
    )
    grad_gu = sum_gu.astype(jnp.bfloat16)
    grad_dn = jnp.swapaxes(sum_dn, 1, 2).astype(jnp.bfloat16)
    return (layer_out, d_tokens, grad_gu, grad_dn)


BF16, F32 = jnp.bfloat16, jnp.float32


def contract(a, b, dim_a, dim_b):
    return lax.dot_general(a, b, (((dim_a,), (dim_b,)), ((), ())), preferred_element_type=F32)


def swap(array, axis, offset):
    size = lax.axis_size(axis)
    return lax.ppermute(array, axis, [(p, p ^ offset) for p in range(size)])


def shift(array, axis, offset):
    size = lax.axis_size(axis)
    return lax.ppermute(array, axis, [(p, (p + offset) % size) for p in range(size)])


def partial_kernel(x_ref, c_ref, gu_ref, dn_ref, *outs):
    peers, _, rows, width = x_ref.shape
    split = gu_ref.shape[2]
    gate_up = contract(x_ref[...].reshape(peers * rows, width), gu_ref[0], 1, 0)
    d_act = contract(c_ref[...].reshape(peers * rows, width), dn_ref[0], 1, 1)
    for j, out in enumerate(outs):
        out[0, :, :split] = gate_up[j * rows : (j + 1) * rows].astype(out.dtype)
        out[0, :, split:] = d_act[j * rows : (j + 1) * rows].astype(out.dtype)


def partial_products(x, c, w_gate_up, w_down, first, count):
    peers, _, rows, width = x.shape
    hidden = w_down.shape[1]
    row_spec = pl.BlockSpec((peers, 1, rows, width), lambda s: (0, s + first, 0, 0))
    dtypes = [BF16 if j & 1 else F32 for j in range(peers)]
    return pl.pallas_call(
        partial_kernel,
        grid=(count,),
        in_specs=[
            row_spec,
            row_spec,
            pl.BlockSpec((1, width, 2 * hidden), lambda s: (s + first, 0, 0)),
            pl.BlockSpec((1, hidden, width), lambda s: (s + first, 0, 0)),
        ],
        out_specs=[pl.BlockSpec((1, rows, 3 * hidden), lambda s: (s, 0, 0)) for _ in dtypes],
        out_shape=[jax.ShapeDtypeStruct((count, rows, 3 * hidden), t) for t in dtypes],
        cost_estimate=pl.CostEstimate(
            flops=2 * count * peers * rows * width * 3 * hidden,
            bytes_accessed=count * (3 * hidden * width * 2 + peers * rows * (3 * hidden * 3 + width * 4)),
            transcendentals=0,
        ),
    )(x, c, w_gate_up, w_down)


def back_kernel(*refs):
    *mids, gate_ref, gu_ref, dn_ref, out_ref, grad_ref = refs
    hidden = dn_ref.shape[1]
    mid = jnp.concatenate([m[0] for m in mids], axis=0)
    out = contract(mid[:, :hidden], dn_ref[0], 1, 0)
    out_ref[0] = (gate_ref[0] * out).astype(BF16)
    grad_ref[0] = contract(mid[:, hidden:], gu_ref[0], 1, 1).astype(BF16)


def back_products(mids, gates, w_gate_up, w_down, first):
    count, rows, wide = mids[0].shape
    hidden, width = w_down.shape[1:]
    total = rows * len(mids)
    out_spec = pl.BlockSpec((1, total, width), lambda s: (s, 0, 0))
    return pl.pallas_call(
        back_kernel,
        grid=(count,),
        in_specs=[pl.BlockSpec((1, rows, wide), lambda s: (s, 0, 0)) for _ in mids]
        + [
            pl.BlockSpec((1, total, 1), lambda s: (s + first, 0, 0)),
            pl.BlockSpec((1, width, 2 * hidden), lambda s: (s + first, 0, 0)),
            pl.BlockSpec((1, hidden, width), lambda s: (s + first, 0, 0)),
        ],
        out_specs=[out_spec, out_spec],
        out_shape=[jax.ShapeDtypeStruct((count, total, width), BF16)] * 2,
        cost_estimate=pl.CostEstimate(
            flops=2 * count * total * width * wide,
            bytes_accessed=count * 2 * (wide * width + total * (wide + 2 * width)),
            transcendentals=0,
        ),
    )(*mids, gates, w_gate_up, w_down)


def combine_kernel(one_ref, out_ref, grad_ref, sum_ref):
    slots, most, tokens = one_ref.shape[2:]
    one = one_ref[...].reshape(slots * most, tokens)
    width = out_ref.shape[-1]
    sum_ref[0, 0, 0] = contract(one, out_ref[...].reshape(slots * most, width), 0, 0).astype(BF16)
    sum_ref[0, 0, 1] = contract(one, grad_ref[...].reshape(slots * most, width), 0, 0).astype(BF16)


def combine(one, out_rows, grad_rows):
    far, near, slots, most, tokens = one.shape
    width = out_rows.shape[-1]
    shape = (slots, near, far, most, width)
    row_spec = pl.BlockSpec((slots, 1, 1, most, width), lambda k, j: (0, j, k, 0, 0))
    return pl.pallas_call(
        combine_kernel,
        grid=(far, near),
        in_specs=[
            pl.BlockSpec((1, 1, slots, most, tokens), lambda k, j: (k, j, 0, 0, 0)),
            row_spec,
            row_spec,
        ],
        out_specs=pl.BlockSpec((1, 1, 2, tokens, width), lambda k, j: (k, j, 0, 0, 0)),
        out_shape=jax.ShapeDtypeStruct((far, near, 2, tokens, width), BF16),
    )(one, out_rows.reshape(shape), grad_rows.reshape(shape))


def grads_kernel(x_ref, c_ref, *refs):
    *mids, gu_ref, dn_ref = refs
    peers, _, rows, width = x_ref.shape
    hidden = dn_ref.shape[1]
    mid = jnp.concatenate([m[0] for m in mids], axis=0)
    gu_ref[0] = contract(x_ref[...].reshape(peers * rows, width), mid[:, hidden:], 0, 0).astype(BF16)
    dn_ref[0] = contract(mid[:, :hidden], c_ref[...].reshape(peers * rows, width), 0, 0).astype(BF16)


def weight_grads(x, c, mids):
    peers, slots, rows, width = x.shape
    most, wide = mids[0].shape[1:]
    hidden = wide // 3
    row_spec = pl.BlockSpec((peers, 1, rows, width), lambda s: (0, s, 0, 0))
    return pl.pallas_call(
        grads_kernel,
        grid=(slots,),
        in_specs=[row_spec, row_spec]
        + [pl.BlockSpec((1, most, wide), lambda s: (s, 0, 0)) for _ in mids],
        out_specs=[
            pl.BlockSpec((1, width, 2 * hidden), lambda s: (s, 0, 0)),
            pl.BlockSpec((1, hidden, width), lambda s: (s, 0, 0)),
        ],
        out_shape=[
            jax.ShapeDtypeStruct((slots, width, 2 * hidden), BF16),
            jax.ShapeDtypeStruct((slots, hidden, width), BF16),
        ],
    )(x, c, *mids)


def route(ids, gates, chosen):
    tokens = ids.shape[-1]
    match = ids[:, :, None] == chosen[None, None, :, None, None]
    hit = jnp.any(match, axis=3)
    gate = jnp.sum(jnp.where(match, gates[:, :, None], 0.0), axis=3)
    earlier = jnp.triu(jnp.ones((tokens, tokens), BF16), 1)
    place = jnp.einsum("kjst,tu->kjsu", hit.astype(BF16), earlier, preferred_element_type=F32)
    cell = jnp.arange(MOST, dtype=jnp.int32)[None, None, None, :, None]
    one = hit[:, :, :, None] & (place.astype(jnp.int32)[:, :, :, None] == cell)
    row_gate = jnp.sum(jnp.where(one, gate[:, :, :, None], 0.0), axis=-1)
    return one.astype(BF16), row_gate.transpose(2, 1, 0, 3)


def select(one, row_gate, tokens, cotangent):
    far, near, slots, most, _ = one.shape
    shape = (near, slots, far * most, tokens.shape[-1])
    x = jnp.einsum("kjsmt,kjtd->jskmd", one, tokens, preferred_element_type=F32).astype(BF16)
    c = jnp.einsum("kjsmt,kjtd->jskmd", one, cotangent, preferred_element_type=F32)
    c = (row_gate.swapaxes(0, 1)[..., None] * c).astype(BF16)
    return x.reshape(shape), c.reshape(shape)


def by_slices(tokens, expert_ids, gate_values, w_gate_up, w_down, new_slot, cotangent, chunks=1):
    far, near = lax.axis_size("expert"), lax.axis_size("dp")
    here, lane = lax.axis_index("expert"), lax.axis_index("dp")
    slots, width, wide = w_gate_up.shape
    hidden = wide // 2
    count, top = expert_ids.shape
    bits = [1 << b for b in range(near.bit_length() - 1)]

    info = jnp.concatenate([expert_ids.T.astype(F32), gate_values.T], axis=0)
    info = lax.all_gather(info, ("expert", "dp"), axis=0)
    order = (here - jnp.arange(far)[:, None]) % far * near + (lane ^ jnp.arange(near)[None, :])
    info = info[order]
    ids, gates = info[:, :, :top].astype(jnp.int32), info[:, :, top:]

    pair = jnp.stack([tokens, cotangent]).reshape(2, count, near, width).transpose(2, 0, 1, 3)
    pieces = []
    for j in range(near):
        piece = lax.dynamic_index_in_dim(pair, lane ^ j, 0, keepdims=False)
        pieces.append(swap(piece, "dp", j) if j else piece)
    blocks = [jnp.stack(pieces)]
    for _ in range(far - 1):
        blocks.append(shift(blocks[-1], "expert", 1))
    blocks = jnp.stack(blocks)
    all_tokens, all_cot = blocks[:, :, 0], blocks[:, :, 1]

    one, row_gate = route(ids, gates, here * slots + jnp.arange(slots))
    x, c = select(one, row_gate, all_tokens, all_cot)
    gate_column = row_gate.reshape(slots, near * far * MOST, 1)

    step = slots // chunks
    home = [[None] * chunks for _ in range(far)]
    out_rows, grad_rows = [], []
    for n in range(chunks):
        parts = list(partial_products(x, c, w_gate_up, w_down, n * step, step))
        for bit in bits:
            for j in range(0, near, 2 * bit):
                got = swap(parts[j + bit].astype(BF16), "dp", bit)
                parts[j] = parts[j].astype(F32) + got.astype(F32)
        gate, up, d_act = (parts[0][..., p * hidden : (p + 1) * hidden] for p in range(3))
        sigmoid = jax.nn.sigmoid(gate)
        silu = gate * sigmoid
        mid = jnp.concatenate(
            [silu * up, d_act * up * sigmoid * (1.0 + gate * (1.0 - sigmoid)), d_act * silu],
            axis=-1,
        ).astype(BF16)
        by_home = mid.reshape(step, far, MOST, 3 * hidden)
        for k in range(far):
            home[k][n] = shift(by_home[:, k], "expert", -k) if k else by_home[:, k]
        mids = {0: mid}
        for bit in reversed(bits):
            for j in list(mids):
                mids[j + bit] = swap(mids[j], "dp", bit)
        mids = [mids[j] for j in range(near)]
        out, grad = back_products(mids, gate_column, w_gate_up, w_down, n * step)
        out_rows.append(out)
        grad_rows.append(grad)

    held = jnp.concatenate([home[k][n] for k in range(far) for n in range(chunks)], axis=0)
    experts = far * slots
    numbers = jnp.arange(experts, dtype=jnp.int32)
    inverse = jnp.sum(jnp.where(new_slot[None, :] == numbers[:, None], numbers[None, :], 0), axis=1)
    moved = {}
    for k in range(far):
        chosen = inverse[(here + k) % far * slots + jnp.arange(slots)]
        place = (chosen // slots - here) % far * slots + chosen % slots
        picked = held[place]
        moved[k, 0] = shift(picked, "expert", k) if k else picked
    for bit in reversed(bits):
        for k, j in list(moved):
            moved[k, j + bit] = swap(moved[k, j], "dp", bit)

    one_new, gate_new = route(ids, gates, inverse[here * slots + jnp.arange(slots)])
    x_new, c_new = select(one_new, gate_new, all_tokens, all_cot)
    d_gate_up, d_down = weight_grads(
        x_new, c_new, [moved[k, j] for j in range(near) for k in range(far)]
    )

    sums = combine(one, jnp.concatenate(out_rows), jnp.concatenate(grad_rows))
    total = sums[1 % far]
    for k in range(1, far):
        got = shift(total, "expert", 1)
        total = (got.astype(F32) + sums[(k + 1) % far].astype(F32)).astype(BF16)
    pieces = [swap(total[j], "dp", j) if j else total[j] for j in range(near)]
    whole = jnp.stack(pieces)[lane ^ jnp.arange(near)]
    whole = whole.transpose(1, 2, 0, 3).reshape(2, count, near * width)
    return whole[0], whole[1], d_gate_up, d_down


def shards(tokens, expert_ids, *rest):
    far, near = lax.axis_size("expert"), lax.axis_size("dp")
    if far <= expert_ids.shape[1] and near & (near - 1) == 0:
        return by_slices(tokens, expert_ids, *rest)
    return by_rows(tokens, expert_ids, *rest)


def solution(mesh):
    return jax.shard_map(
        shards,
        mesh=mesh,
        in_specs=(
            P(("groups", "expert", "dp"), None),
            P(("groups", "expert", "dp"), None),
            P(("groups", "expert", "dp"), None),
            P("expert", "dp", None),
            P("expert", None, "dp"),
            P(),
            P(("groups", "expert", "dp"), None),
        ),
        out_specs=(
            P(("groups", "expert", "dp"), None),
            P(("groups", "expert", "dp"), None),
            P(("groups", "expert"), "dp", None),
            P(("groups", "expert"), None, "dp"),
        ),
        check_vma=False,
    )
```
